128 devices in a mesh: tgt: 16 (over z_lo, y, core), src: 8 (over x, z_hi).
Axes of the slice: x: 4, y: 4, z: 4 (z_hi: 2, z_lo: 2; z = z_hi * 2 + z_lo), core: 2. Of those that a mesh axis runs over, the one named last changes fastest.
Arguments:
- targets: float32 [16, 64, 4096], P('tgt'), may hold values from -8 to 8
- sources: float32 [16, 64, 4096], P('src', 'tgt'), may hold values from -8 to 8
- occupations: float32 [16], P('src'), may hold values from 0.2 to 2
Outputs:
- exchange_term: float32 [16, 64, 4096], P('tgt', 'src')
The draws below stay inside these ranges and needn't reach their ends.
All inputs are finite; a program needn't handle non-finite values.
Results may differ from the reference program's by a relative error of at most 0.000076.
Values sent between devices are 32-bit elements; how exact they have to be, the bound alone decides.
No kernel may reach another device: no remote copies, remote signals or barrier semaphores. Data moves between devices by JAX's collectives and lax.ppermute only.
A program may use at most 64 MiB of HBM per device.

```python
import math
import jax
import jax.numpy as jnp
from jax import lax

G = 64
NT = 16
NS = 16


def orbital_field(key, count, salt):
    key = jax.random.fold_in(key, salt)
    first, second = jax.random.split(key, 2)
    scales = jnp.exp(jax.random.uniform(first, (count, 1, 1), jnp.float32, math.log(0.5), math.log(2.0)))
    rough = jax.random.normal(second, (count, G, G * G), jnp.float32) * scales
    return jnp.clip(rough, -8.0, 8.0).astype(jnp.float32)


def draw_targets(key, part):
    return orbital_field(key, NT, 11)


def draw_sources(key, part):
    return orbital_field(key, NS, 23)


def block_scale(stream_key, extent, cuts, least, largest):
    gain, own = 1.0, jax.random.fold_in(stream_key, 6)
    for axis_at, shards_of in cuts:
        steps = jnp.exp(jax.random.uniform(jax.random.fold_in(own, axis_at), (shards_of,), jnp.float32, least / len(cuts), largest / len(cuts)))
        gain = gain * jnp.repeat(steps, extent[axis_at] // shards_of).reshape([-1 if axis == axis_at else 1 for axis in range(len(extent))])
    return gain


def setup_inputs(seed: int = 0) -> dict:
    streams_of = jax.random.split(jax.random.key(seed), 4)
    return {
        "targets": draw_targets(jax.random.fold_in(streams_of[3], 71), 0),
        "sources": draw_sources(jax.random.fold_in(streams_of[3], 71), 0),
        "occupations": jnp.clip(jnp.exp(math.log(2.0) - 2.3025851 * jax.random.uniform(streams_of[2], (NS,), jnp.float32) ** block_scale(streams_of[2], (NS,), ((0, 8),), -0.2, 0.2)), 0.2, 2.0),
    }


def kernel_grid(size):
    freq = ((jnp.arange(size, dtype=jnp.int32) + size // 2) % size - size // 2).astype(jnp.float32)
    square = freq[:, None, None] ** 2 + freq[None, :, None] ** 2 + freq[None, None, :] ** 2
    return 16.0 / (square + 0.25)


def reference(targets, sources, occupations):
    size = targets.shape[1]
    count = sources.shape[0]
    kernel = kernel_grid(size)
    source_grid = sources.reshape(count, size, size, size)
    weighted = occupations[:, None, None, None] * source_grid

    def one_target(target):
        pair = target.reshape(size, size, size)[None] * source_grid
        spectrum = jnp.fft.fftn(pair, axes=(1, 2, 3))
        potential = jnp.real(jnp.fft.ifftn(kernel[None] * spectrum, axes=(1, 2, 3)))
        total = -jnp.sum(weighted * potential, axis=0)
        return total.reshape(size, size * size)

    return lax.map(one_target, targets)
```

```python
import functools

import jax
import jax.numpy as jnp
import numpy as np
from jax import lax
from jax.experimental import pallas as pl
from jax.experimental.pallas import tpu as pltpu
from jax.sharding import PartitionSpec as P

N = 64
H = 32
L = 128
PAIRS = N // 2


def real_basis():
    n = np.arange(N)
    rows = [np.ones(N)]
    for k in range(1, N // 2):
        rows.append(np.sqrt(2.0) * np.cos(2 * np.pi * k * n / N))
    rows.append((-1.0) ** n)
    for k in range(1, N // 2):
        rows.append(np.sqrt(2.0) * np.sin(2 * np.pi * k * n / N))
    freq = np.array(list(range(0, N // 2 + 1)) + list(range(1, N // 2)), np.float64)
    return np.array(rows) / np.sqrt(N), freq


def halves(table):
    high = table.astype(jnp.bfloat16)
    low = (table - high.astype(np.float64)).astype(jnp.bfloat16)
    return high, low


def left_table(matrix):
    high, low = halves(matrix)
    return np.concatenate([high, high, low, low], axis=1)


def right_table(matrix):
    block = np.zeros((L, L))
    block[:N, :N] = matrix
    block[N:, N:] = matrix
    high, low = halves(block)
    both = np.concatenate([high, low], axis=1)
    return np.concatenate([both, both], axis=0)


BASIS, FREQ = real_basis()
ORDER = np.concatenate([np.arange(0, N, 2), np.arange(1, N, 2)])
BASIS_Y = BASIS[:, ORDER]


def split(value):
    high = value.astype(jnp.bfloat16)
    low = (value - high.astype(jnp.float32)).astype(jnp.bfloat16)
    return high, low


def stacked(value):
    high, low = split(value)
    return jnp.concatenate([high, low, high, low], axis=0)


def dot(left, right):
    return jnp.dot(left, right, preferred_element_type=jnp.float32)


def from_left(table, first, second):
    both = jnp.concatenate([stacked(first), stacked(second)], axis=1)
    out = dot(table, both)
    return out[:, :L], out[:, L:]


def from_right(value, table):
    high, low = split(value)
    out = dot(jnp.concatenate([high, low], axis=1), table)
    return out[:, :L] + out[:, L:]


def exchange_kernel(s_ref, t_ref, k_ref, w_ref, ly, lx, ix, iy, rz, qz, out_ref, one, two):
    def forward(i, _):
        fields = []
        for e in range(2):
            x = 2 * i + e
            fields.append(from_right(t_ref[x] * s_ref[x], rz[...]))
        a, b = from_left(ly[...], *fields)
        one[pl.ds(pl.multiple_of(2 * i * N, N), N), :] = a
        one[pl.ds(pl.multiple_of((2 * i + 1) * N, N), N), :] = b
        return 0

    lax.fori_loop(0, PAIRS, forward, 0, unroll=4)

    def middle(i, _):
        first = one[pl.ds(2 * i, N, stride=N), :]
        second = one[pl.ds(2 * i + 1, N, stride=N), :]
        a, b = from_left(lx[...], first, second)
        a = a * k_ref[2 * i]
        b = b * k_ref[2 * i + 1]
        a, b = from_left(ix[...], a, b)
        two[pl.ds(2 * i, N, stride=N), :] = a
        two[pl.ds(2 * i + 1, N, stride=N), :] = b
        return 0

    lax.fori_loop(0, PAIRS, middle, 0, unroll=4)

    lane = lax.broadcasted_iota(jnp.int32, (H, L), 1) < N

    def backward(i, _):
        first = two[pl.ds(pl.multiple_of(2 * i * N, N), N), :]
        second = two[pl.ds(pl.multiple_of((2 * i + 1) * N, N), N), :]
        fields = from_left(iy[...], first, second)
        for e in range(2):
            x = 2 * i + e
            v = from_right(fields[e], qz[...]) * s_ref[x] * w_ref[...]
            even, odd = v[:H], v[H:]
            kept = jnp.where(lane, even, odd)
            moved = jnp.where(lane, odd, even)
            out_ref[x] = kept + pltpu.roll(moved, N, axis=1)
        return 0

    lax.fori_loop(0, PAIRS, backward, 0, unroll=4)


def exchange(s, t, k, w):
    tables = (
        left_table(BASIS_Y),
        left_table(BASIS),
        left_table(BASIS.T),
        left_table(BASIS_Y.T),
        right_table(BASIS.T),
        right_table(BASIS),
    )
    return pl.pallas_call(
        exchange_kernel,
        out_shape=jax.ShapeDtypeStruct((N, H, L), jnp.float32),
        scratch_shapes=[pltpu.VMEM((N * N, L), jnp.float32), pltpu.VMEM((N * N, L), jnp.float32)],
        name="exchange",
    )(s, t, k, w, *[jnp.asarray(v) for v in tables])


def kernel_grid():
    freq = jnp.asarray(FREQ, jnp.float32) ** 2
    square = freq[:, None, None] + freq[None, :, None] + freq[None, None, :]
    base = 16.0 / (square + 0.25)
    return jnp.concatenate([base, base], axis=-1)


def on_device(targets, sources, occupations):
    w = -jnp.repeat(occupations, N).reshape(1, L)
    packed = sources.reshape(2, 4, H, 2, N).transpose(1, 3, 2, 0, 4).reshape(4, N, L)
    copies = jnp.broadcast_to(packed, (16, 4, N, L))
    whole = lax.all_to_all(copies, "tgt", split_axis=0, concat_axis=0, tiled=True)
    whole = whole.reshape(N, N, L)
    t = targets.reshape(N, H, 2, N).transpose(0, 2, 1, 3).reshape(N, N, N)
    t = jnp.concatenate([t, t], axis=-1)
    part = exchange(whole, t, kernel_grid(), w)
    tiles = part.reshape(8, 8, H, L)
    arrived = lax.all_to_all(tiles, "src", split_axis=0, concat_axis=0, tiled=True)
    return arrived.sum(axis=0).reshape(1, 8, H * L)


def solution(mesh):
    return jax.shard_map(
        on_device,
        mesh=mesh,
        in_specs=(P("tgt", None, None), P("src", "tgt", None), P("src")),
        out_specs=P("tgt", "src", None),
        check_vma=False,
    )
```

```python
import functools

import jax
import jax.numpy as jnp
import numpy as np
from jax import lax
from jax.experimental import pallas as pl
from jax.experimental.pallas import tpu as pltpu
from jax.sharding import PartitionSpec as P

N = 64
H = 32
L = 128
PITCH = N + 2
BLOCK = 16
CHUNK = 2 * H * 4
SLAB = H * 8
EARLY = 10


def real_basis():
    n = np.arange(N)
    rows = [np.ones(N)]
    for k in range(1, N // 2):
        rows.append(np.sqrt(2.0) * np.cos(2 * np.pi * k * n / N))
    rows.append((-1.0) ** n)
    for k in range(1, N // 2):
        rows.append(np.sqrt(2.0) * np.sin(2 * np.pi * k * n / N))
    freq = np.array(list(range(0, N // 2 + 1)) + list(range(1, N // 2)), np.float64)
    return np.array(rows) / np.sqrt(N), freq


def halves(table):
    high = table.astype(jnp.bfloat16)
    low = (table - high.astype(np.float64)).astype(jnp.bfloat16)
    return high, low


def left_table(matrix):
    high, low = halves(matrix)
    return np.concatenate([high, high, low], axis=1)


def right_table(matrix):
    block = np.zeros((L, L))
    block[:N, :N] = matrix
    block[N:, N:] = matrix
    high, low = halves(block)
    both = np.concatenate([high, low], axis=1)
    return np.concatenate([both, both], axis=0)


BASIS, FREQ = real_basis()
ORDER = np.concatenate([np.arange(0, N, 2), np.arange(1, N, 2)])
BASIS_Y = BASIS[:, ORDER]


def split(value):
    high = value.astype(jnp.bfloat16)
    low = (value - high.astype(jnp.float32)).astype(jnp.bfloat16)
    return high, low


def dot(left, right):
    return jnp.dot(left, right, preferred_element_type=jnp.float32)


def stacked(value):
    high, low = split(value)
    return jnp.concatenate([high, low, high], axis=0)


def from_left(table, first, second):
    out = dot(table, jnp.concatenate([stacked(first), stacked(second)], axis=1))
    return out[:, :L], out[:, L:]


def from_right(value, table):
    high, low = split(value)
    out = dot(jnp.concatenate([high, low], axis=1), table)
    return out[:, :L] + out[:, L:]


def pipelined(first, second, count, buffers):
    first(0, buffers[0])
    for n in range(1, count):
        first(n, buffers[n % 2])
        second(n - 1, buffers[(n - 1) % 2])
    second(count - 1, buffers[(count - 1) % 2])


def lane_mask():
    return lax.broadcasted_iota(jnp.int32, (H, L), 1) < N


def mixed(first, second, lane):
    low = jnp.where(lane, first, pltpu.roll(second, N, axis=1))
    high = jnp.where(lane, pltpu.roll(first, N, axis=1), second)
    return low, high


def pair_plane(chunk, t_ref, s_ref, x, e, lane):
    a = chunk[pl.ds(e, H, stride=4), :]
    b = chunk[pl.ds(CHUNK // 2 + e, H, stride=4), :]
    low, high = mixed(a, b, lane)
    s_ref[x, 0:H] = low
    s_ref[x, H:N] = high
    t = t_ref[pl.ds((x // 8) * SLAB + x % 8, H, stride=8), :]
    moved = pltpu.roll(t, N, axis=1)
    return jnp.concatenate(
        [low * jnp.where(lane, t, moved), high * jnp.where(lane, moved, t)], axis=0
    )


def near_transforms(chunks, starts, t_ref, s_ref, one, held, ly, rz):
    lane = lane_mask()
    group = 2

    def depth(n, buffer):
        planes = []
        for c in range(group * n, group * (n + 1)):
            for e in range(4):
                planes.append(pair_plane(chunks(c), t_ref, s_ref, starts[c] + e, e, lane))
        buffer[0 : group * 4 * N] = from_right(jnp.concatenate(planes, axis=0), rz[...])

    def rows(n, buffer):
        for e in range(0, group * 4, 2):
            x = starts[group * n + e // 4] + e % 4
            a, b = from_left(ly[...], buffer[e * N : (e + 1) * N], buffer[(e + 1) * N : (e + 2) * N])
            one[pl.ds(x * PITCH, N), :] = a
            one[pl.ds((x + 1) * PITCH, N), :] = b

    pipelined(depth, rows, len(starts) // group, held)


def early_kernel(starts_ref, *refs):
    chunks, (t_ref, ly, rz, s_ref, one, *held) = refs[:EARLY], refs[EARLY:]
    starts = [starts_ref[c] for c in range(EARLY)]
    near_transforms(lambda c: chunks[c], starts, t_ref, s_ref, one, held, ly, rz)


def late_kernel(starts_ref, slabs_ref, w_ref, *refs):
    late = 16 - EARLY
    chunks, refs = refs[:late], refs[late:]
    t_ref, s_in, one_in, k_in, ly, lx, ix, iy, rz, qz = refs[:10]
    outs, (s_ref, one, two, k_ref, sems, *held) = refs[10:18], refs[18:]
    copies = []
    for c in range(EARLY):
        x = pl.multiple_of(starts_ref[c], 4)
        rows = pl.ds(pl.multiple_of(x * PITCH, 8), 4 * PITCH)
        copies.append(pltpu.make_async_copy(one_in.at[rows], one.at[rows], sems.at[2 * c]))
        planes = pl.ds(x, 4)
        copies.append(pltpu.make_async_copy(s_in.at[planes], s_ref.at[planes], sems.at[2 * c + 1]))
    copies.append(pltpu.make_async_copy(k_in, k_ref, sems.at[2 * EARLY]))
    for copy in copies:
        copy.start()
    starts = [starts_ref[EARLY + c] for c in range(late)]
    near_transforms(lambda c: chunks[c], starts, t_ref, s_ref, one, held, ly, rz)
    for copy in copies:
        copy.wait()

    def planes(n, buffer):
        for e in range(0, BLOCK, 2):
            y = BLOCK * n + e
            a, b = from_left(
                lx[...],
                one[pl.ds(y, N, stride=PITCH), :],
                one[pl.ds(y + 1, N, stride=PITCH), :],
            )
            buffer[e * N : (e + 1) * N] = a * k_ref[y]
            buffer[(e + 1) * N : (e + 2) * N] = b * k_ref[y + 1]

    def planes_back(n, buffer):
        for e in range(0, BLOCK, 2):
            y = BLOCK * n + e
            a, b = from_left(ix[...], buffer[e * N : (e + 1) * N], buffer[(e + 1) * N : (e + 2) * N])
            two[pl.ds(y * PITCH, N), :] = a
            two[pl.ds((y + 1) * PITCH, N), :] = b

    pipelined(planes, planes_back, N // BLOCK, held)

    lane = lane_mask()
    slabs = [slabs_ref[c] * 8 for c in range(8)]

    def rows_back(n, buffer):
        for e in range(0, BLOCK, 2):
            x = slabs[(BLOCK * n + e) // 8] + e % 8
            a, b = from_left(
                iy[...], two[pl.ds(x, N, stride=PITCH), :], two[pl.ds(x + 1, N, stride=PITCH), :]
            )
            buffer[e * N : (e + 1) * N] = a
            buffer[(e + 1) * N : (e + 2) * N] = b

    def depth_back(n, buffer):
        field = from_right(buffer[...], qz[...])
        for e in range(BLOCK):
            slab = (BLOCK * n + e) // 8
            v = field[e * N : (e + 1) * N] * s_ref[slabs[slab] + e % 8] * w_ref[...]
            low, high = v[:H], v[H:]
            kept = jnp.where(lane, low, high)
            other = jnp.where(lane, high, low)
            outs[slab][pl.ds(e % 8, H, stride=8), :] = kept + pltpu.roll(other, N, axis=1)

    pipelined(rows_back, depth_back, N // BLOCK, held)


def f32(*shape):
    return jax.ShapeDtypeStruct(shape, jnp.float32)


HELD = [pltpu.VMEM((BLOCK * N, L), jnp.float32)] * 2
SMEM = pl.BlockSpec(memory_space=pltpu.SMEM)
ANY = pl.BlockSpec(memory_space=pl.ANY)
VMEM = pl.BlockSpec(memory_space=pltpu.VMEM)


def early(starts, chunks, t):
    tables = [jnp.asarray(v) for v in (left_table(BASIS_Y), right_table(BASIS.T))]
    return pl.pallas_call(
        early_kernel,
        in_specs=[SMEM] + [VMEM] * (EARLY + 3),
        out_shape=(f32(N, N, L), f32(N * PITCH, L)),
        scratch_shapes=HELD,
        name="early",
    )(starts, *chunks, t, *tables)


def late(starts, slabs, w, chunks, t, s, one, k):
    tables = (
        left_table(BASIS_Y),
        left_table(BASIS),
        left_table(BASIS.T),
        left_table(BASIS_Y.T),
        right_table(BASIS.T),
        right_table(BASIS),
    )
    return pl.pallas_call(
        late_kernel,
        in_specs=[SMEM] * 2 + [VMEM] * (2 + 16 - EARLY) + [ANY] * 3 + [VMEM] * 6,
        out_shape=[f32(SLAB, L)] * 8,
        scratch_shapes=[
            pltpu.VMEM((N, N, L), jnp.float32),
            pltpu.VMEM((N * PITCH, L), jnp.float32),
            pltpu.VMEM((N * PITCH, L), jnp.float32),
            pltpu.VMEM((N, N, L), jnp.float32),
            pltpu.SemaphoreType.DMA((2 * EARLY + 1,)),
            *HELD,
        ],
        name="late",
    )(starts, slabs, w, *chunks, t, s, one, k, *[jnp.asarray(v) for v in tables])


def kernel_grid():
    freq = jnp.asarray(FREQ, jnp.float32) ** 2
    square = freq[:, None, None] + freq[None, :, None] + freq[None, None, :]
    base = 16.0 / (square + 0.25)
    return jnp.concatenate([base, base], axis=-1)


def tgt_move(value, dz, dy, dc):
    pairs = []
    for z in range(2):
        for y in range(4):
            for c in range(2):
                to = ((z + dz) % 2 * 4 + (y + dy) % 4) * 2 + (c + dc) % 2
                pairs.append(((z * 4 + y) * 2 + c, to))
    return lax.ppermute(value, "tgt", pairs)


def src_move(value, dx, dh):
    pairs = []
    for x in range(4):
        for h in range(2):
            pairs.append((x * 2 + h, (x + dx) % 4 * 2 + (h + dh) % 2))
    return lax.ppermute(value, "src", pairs)


def on_device(targets, sources, occupations):
    tgt, src = lax.axis_index("tgt"), lax.axis_index("src")
    z, y, c = tgt // 8, tgt // 2 % 4, tgt % 2
    x, h = src // 2, src % 2

    own = sources.reshape(2, 4, H, L).transpose(0, 2, 1, 3).reshape(CHUNK, L)
    t = targets.reshape(8, 8, H, L).transpose(0, 2, 1, 3).reshape(8 * SLAB, L)
    w = -jnp.repeat(occupations, N).reshape(1, L)

    across = tgt_move(own, 1, 0, 0)
    sent = [own, across] + [tgt_move(own, 0, d, 0) for d in (2, 1, -1)]
    sent += [tgt_move(across, 0, d, 0) for d in (2, 1, -1)]
    other = [tgt_move(v, 0, 0, 1) for v in sent]
    chunks = [v for both in zip(sent, other) for v in both]
    starts = []
    for dz, dy in ((0, 0), (1, 0), (0, 2), (0, -1), (0, 1), (1, 2), (1, -1), (1, 1)):
        for dc in (0, 1):
            starts.append((((z + dz) % 2 * 4 + (y + dy) % 4) * 2 + (c + dc) % 2) * 4)
    starts = jnp.stack(starts).astype(jnp.int32)
    slabs = []
    for dh in (1, 0):
        for dx in (2, 1, -1, 0):
            slabs.append((x + dx) % 4 * 2 + (h + dh) % 2)
    slabs = jnp.stack(slabs).astype(jnp.int32)

    s, one = early(starts, chunks[:EARLY], t)
    parts = late(starts, slabs, w, chunks[EARLY:], t, s, one, kernel_grid())

    arrived = [src_move(parts[n], d, 0) for n, d in enumerate((2, 1, -1))]
    direct = [src_move(parts[4 + n], d, 0) for n, d in enumerate((2, 1, -1))]
    crossed = src_move(sum(arrived, parts[3]), 0, 1)
    total = sum(direct, parts[7]) + crossed
    return total.reshape(H, 8, L).transpose(1, 0, 2).reshape(1, 8, H * L)


def solution(mesh):
    return jax.shard_map(
        on_device,
        mesh=mesh,
        in_specs=(P("tgt", None, None), P("src", "tgt", None), P("src")),
        out_specs=P("tgt", "src", None),
        check_vma=False,
    )
```

```python
import jax
import jax.numpy as jnp
import numpy as np
from jax import lax
from jax.experimental import pallas as pl
from jax.experimental.pallas import tpu as pltpu
from jax.sharding import PartitionSpec as P

N = 64
H = 32
L = 128
PITCH = N + 2
BLOCK = 16
CHUNK = 2 * H * 4
SLAB = H * 8
EARLY = 10


def real_basis():
    n = np.arange(N)
    rows = [np.ones(N)]
    for k in range(1, N // 2):
        rows.append(np.sqrt(2.0) * np.cos(2 * np.pi * k * n / N))
    rows.append((-1.0) ** n)
    for k in range(1, N // 2):
        rows.append(np.sqrt(2.0) * np.sin(2 * np.pi * k * n / N))
    freq = np.array(list(range(0, N // 2 + 1)) + list(range(1, N // 2)), np.float64)
    return np.array(rows) / np.sqrt(N), freq


def halves(table):
    high = table.astype(jnp.bfloat16)
    low = (table - high.astype(np.float64)).astype(jnp.bfloat16)
    return high, low


def left_table(matrix):
    high, low = halves(matrix)
    return np.concatenate([high, high, low], axis=1)


def right_table(matrix):
    block = np.zeros((L, L))
    block[:N, :N] = matrix
    block[N:, N:] = matrix
    high, low = halves(block)
    both = np.concatenate([high, low], axis=1)
    return np.concatenate([both, both], axis=0)


BASIS, _ = real_basis()
ORDER = np.concatenate([np.arange(0, N, 2), np.arange(1, N, 2)])
BASIS_Y = BASIS[:, ORDER]


def split(value):
    high = value.astype(jnp.bfloat16)
    low = (value - high.astype(jnp.float32)).astype(jnp.bfloat16)
    return high, low


def dot(left, right):
    return jnp.dot(left, right, preferred_element_type=jnp.float32)


def stacked(value):
    high, low = split(value)
    return jnp.concatenate([high, low, high], axis=0)


def from_left(table, first, second):
    out = dot(table, jnp.concatenate([stacked(first), stacked(second)], axis=1))
    return out[:, :L], out[:, L:]


def from_right(value, table):
    high, low = split(value)
    out = dot(jnp.concatenate([high, low], axis=1), table)
    return out[:, :L] + out[:, L:]


def pipelined(first, second, count, buffers):
    first(0, buffers[0])
    for n in range(1, count):
        first(n, buffers[n % 2])
        second(n - 1, buffers[(n - 1) % 2])
    second(count - 1, buffers[(count - 1) % 2])


def lane_mask():
    return lax.broadcasted_iota(jnp.int32, (H, L), 1) < N


def mixed(first, second, lane):
    low = jnp.where(lane, first, pltpu.roll(second, N, axis=1))
    high = jnp.where(lane, pltpu.roll(first, N, axis=1), second)
    return low, high


def near_transforms(chunks, starts, t_in, s_ref, one, refs, after=None):
    chunk_ref, t_ref, sems, held, ly, rz = refs
    lane = lane_mask()
    count = len(starts) // 2
    copies = []
    for n in range(count):
        group = pl.ds(pl.multiple_of(starts[2 * n] // 8 * SLAB, SLAB), SLAB)
        wanted = [
            pltpu.make_async_copy(t_in.at[group], t_ref.at[pl.ds(n * SLAB, SLAB)], sems.at[3 * n])
        ]
        for e in range(2):
            c = 2 * n + e
            wanted.append(
                pltpu.make_async_copy(
                    chunks[c], chunk_ref.at[pl.ds(c * CHUNK, CHUNK)], sems.at[3 * n + 1 + e]
                )
            )
        for copy in wanted:
            copy.start()
        copies.append(wanted)

    def depth(n, buffer):
        for copy in copies[n]:
            copy.wait()
        planes = []
        for c in range(2 * n, 2 * n + 2):
            within = starts[c] % 8
            for e in range(4):
                a = chunk_ref[pl.ds(c * CHUNK + e, H, stride=4), :]
                b = chunk_ref[pl.ds(c * CHUNK + CHUNK // 2 + e, H, stride=4), :]
                low, high = mixed(a, b, lane)
                s_ref[starts[c] + e, 0:H] = low
                s_ref[starts[c] + e, H:N] = high
                t = t_ref[pl.ds(n * SLAB + within + e, H, stride=8), :]
                moved = pltpu.roll(t, N, axis=1)
                planes.append(low * jnp.where(lane, t, moved))
                planes.append(high * jnp.where(lane, moved, t))
        buffer[0 : 8 * N] = from_right(jnp.concatenate(planes, axis=0), rz[...])

    def rows(n, buffer):
        for e in range(0, 8, 2):
            x = starts[2 * n + e // 4] + e % 4
            a, b = from_left(ly[...], buffer[e * N : (e + 1) * N], buffer[(e + 1) * N : (e + 2) * N])
            one[pl.ds(x * PITCH, N), :] = a
            one[pl.ds((x + 1) * PITCH, N), :] = b
        if after is not None:
            after(n)

    pipelined(depth, rows, count, held)


SHIFTS = ((0, 0), (1, 0), (0, 2), (0, -1), (0, 1), (1, -1), (1, 1), (1, 2))


def chunk_starts():
    tgt = lax.axis_index("tgt")
    z, y, c = tgt // 8, tgt // 2 % 4, tgt % 2
    starts = []
    for dz, dy in SHIFTS:
        for dc in range(2):
            to = ((z + dz) % 2 * 4 + (y + dy + 4) % 4) * 2 + (c + dc) % 2
            starts.append(to * 4)
    return starts


def slab_starts():
    src = lax.axis_index("src")
    x, h = src // 2, src % 2
    starts = []
    for dh in (1, 0):
        for dx in (2, 1, -1, 0):
            starts.append(((x + dx + 4) % 4 * 2 + (h + dh) % 2) * 8)
    return starts


def saved(starts, s_ref, one, s_out, one_out, sems):
    copies = []
    for c, start in enumerate(starts):
        rows = pl.ds(pl.multiple_of(start * PITCH, 8), 4 * PITCH)
        planes = pl.ds(start, 4)
        copies.append(pltpu.make_async_copy(one.at[rows], one_out.at[rows], sems.at[2 * c]))
        copies.append(
            pltpu.make_async_copy(s_ref.at[planes], s_out.at[planes], sems.at[2 * c + 1])
        )
    return copies


def table_plane(y):
    row = lax.broadcasted_iota(jnp.int32, (N, L), 0)
    lane = lax.broadcasted_iota(jnp.int32, (N, L), 1) % N
    x = jnp.where(row > H, row - H, row).astype(jnp.float32)
    z = jnp.where(lane > H, lane - H, lane).astype(jnp.float32)
    return 16.0 / (x * x + z * z + float(y * y) + 0.25)


def early_kernel(*refs):
    chunks, refs = refs[:EARLY], refs[EARLY:]
    t_in, ly, rz, s_out, one_out, k_out, s_ref, one, k_ref, chunk_ref, t_ref, sems, out_sems = refs[:13]
    held = refs[13:]
    starts = chunk_starts()[:EARLY]
    copies = saved(starts, s_ref, one, s_out, one_out, out_sems)
    count = EARLY // 2
    tables = [
        pltpu.make_async_copy(k_ref.at[pl.ds(y, 1)], k_out.at[pl.ds(y, 1)], out_sems.at[2 * EARLY + y])
        for y in range(H + 1)
    ]

    def after(n):
        for copy in copies[4 * n : 4 * n + 4]:
            copy.start()
        for y in range(n * (H + 1) // count, (n + 1) * (H + 1) // count):
            k_ref[y] = table_plane(y)
            tables[y].start()

    refs = (chunk_ref, t_ref, sems, held, ly, rz)
    near_transforms(chunks, starts, t_in, s_ref, one, refs, after)
    for copy in copies + tables:
        copy.wait()


def late_kernel(w_ref, *refs):
    late = 16 - EARLY
    chunks, refs = refs[:late], refs[late:]
    t_in, s_in, one_in, k_in, ly, lx, ix, iy, rz, qz = refs[:10]
    outs, refs = refs[10:18], refs[18:]
    s_ref, one, two, k_ref, chunk_ref, t_ref, near_sems, sems, *held = refs
    starts = chunk_starts()
    copies = saved(starts[:EARLY], s_in, one_in, s_ref, one, sems)
    copies.append(pltpu.make_async_copy(k_in, k_ref, sems.at[2 * EARLY]))
    for copy in copies:
        copy.start()
    refs = (chunk_ref, t_ref, near_sems, held, ly, rz)
    near_transforms(chunks, starts[EARLY:], t_in, s_ref, one, refs)
    for copy in copies:
        copy.wait()

    def planes(n, buffer):
        for e in range(0, BLOCK, 2):
            y = BLOCK * n + e
            a, b = from_left(
                lx[...],
                one[pl.ds(y, N, stride=PITCH), :],
                one[pl.ds(y + 1, N, stride=PITCH), :],
            )
            buffer[e * N : (e + 1) * N] = a * k_ref[y if y <= H else y - H]
            buffer[(e + 1) * N : (e + 2) * N] = b * k_ref[y + 1 if y < H else y + 1 - H]

    def planes_back(n, buffer):
        for e in range(0, BLOCK, 2):
            y = BLOCK * n + e
            a, b = from_left(ix[...], buffer[e * N : (e + 1) * N], buffer[(e + 1) * N : (e + 2) * N])
            two[pl.ds(y * PITCH, N), :] = a
            two[pl.ds((y + 1) * PITCH, N), :] = b

    pipelined(planes, planes_back, N // BLOCK, held)

    lane = lane_mask()
    slabs = slab_starts()
    weight = jnp.where(lax.broadcasted_iota(jnp.int32, (N, L), 1) < N, -w_ref[0], -w_ref[1])

    def rows_back(n, buffer):
        for e in range(0, BLOCK, 2):
            x = slabs[(BLOCK * n + e) // 8] + e % 8
            a, b = from_left(
                iy[...], two[pl.ds(x, N, stride=PITCH), :], two[pl.ds(x + 1, N, stride=PITCH), :]
            )
            buffer[e * N : (e + 1) * N] = a
            buffer[(e + 1) * N : (e + 2) * N] = b

    def depth_back(n, buffer):
        field = from_right(buffer[...], qz[...])
        for e in range(BLOCK):
            slab = (BLOCK * n + e) // 8
            v = field[e * N : (e + 1) * N] * s_ref[slabs[slab] + e % 8] * weight
            low, high = v[:H], v[H:]
            kept = jnp.where(lane, low, high)
            other = jnp.where(lane, high, low)
            outs[slab][pl.ds(e % 8, H, stride=8), :] = kept + pltpu.roll(other, N, axis=1)

    pipelined(rows_back, depth_back, N // BLOCK, held)


def f32(*shape):
    return jax.ShapeDtypeStruct(shape, jnp.float32)


HELD = [pltpu.VMEM((BLOCK * N, L), jnp.float32)] * 2
SMEM = pl.BlockSpec(memory_space=pltpu.SMEM)
ANY = pl.BlockSpec(memory_space=pltpu.HBM)
VMEM = pl.BlockSpec(memory_space=pltpu.VMEM)


def near_scratch(count):
    return [
        pltpu.VMEM((count * CHUNK, L), jnp.float32),
        pltpu.VMEM((count // 2 * SLAB, L), jnp.float32),
        pltpu.SemaphoreType.DMA((3 * count // 2,)),
    ]


def early(chunks, t):
    tables = [jnp.asarray(v) for v in (left_table(BASIS_Y), right_table(BASIS.T))]
    return pl.pallas_call(
        early_kernel,
        in_specs=[ANY] * (EARLY + 1) + [VMEM] * 2,
        out_specs=[ANY] * 3,
        out_shape=(f32(N, N, L), f32(N * PITCH, L), f32(H + 1, N, L)),
        scratch_shapes=[
            pltpu.VMEM((N, N, L), jnp.float32),
            pltpu.VMEM((N * PITCH, L), jnp.float32),
            pltpu.VMEM((H + 1, N, L), jnp.float32),
            *near_scratch(EARLY),
            pltpu.SemaphoreType.DMA((2 * EARLY + H + 1,)),
            *HELD,
        ],
        name="early",
    )(*chunks, t, *tables)


def late(w, chunks, t, s, one, k):
    tables = (
        left_table(BASIS_Y),
        left_table(BASIS),
        left_table(BASIS.T),
        left_table(BASIS_Y.T),
        right_table(BASIS.T),
        right_table(BASIS),
    )
    return pl.pallas_call(
        late_kernel,
        in_specs=[SMEM] + [ANY] * (4 + 16 - EARLY) + [VMEM] * 6,
        out_shape=[f32(SLAB, L)] * 8,
        scratch_shapes=[
            pltpu.VMEM((N, N, L), jnp.float32),
            pltpu.VMEM((N * PITCH, L), jnp.float32),
            pltpu.VMEM((N * PITCH, L), jnp.float32),
            pltpu.VMEM((H + 1, N, L), jnp.float32),
            *near_scratch(16 - EARLY),
            pltpu.SemaphoreType.DMA((2 * EARLY + 1,)),
            *HELD,
        ],
        name="late",
    )(w, *chunks, t, s, one, k, *[jnp.asarray(v) for v in tables])


def tgt_move(value, dz, dy, dc):
    pairs = []
    for z in range(2):
        for y in range(4):
            for c in range(2):
                to = ((z + dz) % 2 * 4 + (y + dy) % 4) * 2 + (c + dc) % 2
                pairs.append(((z * 4 + y) * 2 + c, to))
    return lax.ppermute(value, "tgt", pairs)


def src_move(value, dx, dh):
    pairs = []
    for x in range(4):
        for h in range(2):
            pairs.append((x * 2 + h, (x + dx) % 4 * 2 + (h + dh) % 2))
    return lax.ppermute(value, "src", pairs)


def on_device(targets, sources, occupations):
    own = sources.reshape(2, 4, H, L).transpose(0, 2, 1, 3).reshape(CHUNK, L)
    t = targets.reshape(8, 8, H, L).transpose(0, 2, 1, 3).reshape(8 * SLAB, L)

    across = tgt_move(own, 1, 0, 0)
    far, up, down = (
        tgt_move(own, 0, d, 0) for d in (2, 1, -1)
    )
    sent = [own, across, far, up, down]
    sent += [tgt_move(across, 0, d, 0) for d in (1, -1)]
    sent += [tgt_move(far, 1, 0, 0)]
    other = [tgt_move(v, 0, 0, 1) for v in sent]
    chunks = [v for both in zip(sent, other) for v in both]
    s, one, k = early(chunks[:EARLY], t)
    parts = late(occupations, chunks[EARLY:], t, s, one, k)

    far = src_move(parts[0], 0, 1)
    up = src_move(parts[1], 1, 0)
    down = src_move(parts[2], -1, 0)
    near = [src_move(parts[5], 1, 0), src_move(parts[6], -1, 0)]
    near.append(src_move(parts[4] + far, 2, 0))
    crossed = src_move(parts[3] + up + down, 0, 1)
    total = lax.optimization_barrier(sum(near, parts[7])) + crossed
    return total.reshape(H, 8, L).transpose(1, 0, 2).reshape(1, 8, H * L)


def solution(mesh):
    return jax.shard_map(
        on_device,
        mesh=mesh,
        in_specs=(P("tgt", None, None), P("src", "tgt", None), P("src")),
        out_specs=P("tgt", "src", None),
        check_vma=False,
    )
```

```python
import jax
import jax.numpy as jnp
import numpy as np
from jax import lax
from jax.experimental import pallas as pl
from jax.experimental.pallas import tpu as pltpu
from jax.sharding import PartitionSpec as P

N = 64
H = 32
L = 128
PITCH = N + 2
BLOCK = 16
CHUNK = 2 * H * 4
SLAB = H * 8


def real_basis():
    n = np.arange(N)
    rows = [np.ones(N)]
    for k in range(1, N // 2):
        rows.append(np.sqrt(2.0) * np.cos(2 * np.pi * k * n / N))
    rows.append((-1.0) ** n)
    for k in range(1, N // 2):
        rows.append(np.sqrt(2.0) * np.sin(2 * np.pi * k * n / N))
    freq = np.array(list(range(0, N // 2 + 1)) + list(range(1, N // 2)), np.float64)
    return np.array(rows) / np.sqrt(N), freq


def halves(table):
    high = table.astype(jnp.bfloat16)
    low = (table - high.astype(np.float64)).astype(jnp.bfloat16)
    return high, low


def left_table(matrix):
    high, low = halves(matrix)
    return np.concatenate([high, high, low], axis=1)


def right_table(matrix):
    block = np.zeros((L, L))
    block[:N, :N] = matrix
    block[N:, N:] = matrix
    high, low = halves(block)
    both = np.concatenate([high, low], axis=1)
    return np.concatenate([both, both], axis=0)


BASIS, _ = real_basis()
ORDER = np.concatenate([np.arange(0, N, 2), np.arange(1, N, 2)])
BASIS_Y = BASIS[:, ORDER]


def split(value):
    high = value.astype(jnp.bfloat16)
    low = (value - high.astype(jnp.float32)).astype(jnp.bfloat16)
    return high, low


def dot(left, right):
    return jnp.dot(left, right, preferred_element_type=jnp.float32)


def stacked(value):
    high, low = split(value)
    return jnp.concatenate([high, low, high], axis=0)


def from_left(table, first, second):
    out = dot(table, jnp.concatenate([stacked(first), stacked(second)], axis=1))
    return out[:, :L], out[:, L:]


def from_right(value, table):
    high, low = split(value)
    out = dot(jnp.concatenate([high, low], axis=1), table)
    return out[:, :L] + out[:, L:]


def pipelined(first, second, count, buffers):
    first(0, buffers[0])
    for n in range(1, count):
        first(n, buffers[n % 2])
        second(n - 1, buffers[(n - 1) % 2])
    second(count - 1, buffers[(count - 1) % 2])


def lane_mask():
    return lax.broadcasted_iota(jnp.int32, (H, L), 1) < N


def mixed(first, second, lane):
    low = jnp.where(lane, first, pltpu.roll(second, N, axis=1))
    high = jnp.where(lane, pltpu.roll(first, N, axis=1), second)
    return low, high


def near_transforms(chunks, starts, t_ref, s_ref, one, held, ly, rz):
    lane = lane_mask()

    def depth(n, buffer):
        planes = []
        for c in range(2 * n, 2 * n + 2):
            for e in range(4):
                a = chunks[c][pl.ds(e, H, stride=4), :]
                b = chunks[c][pl.ds(CHUNK // 2 + e, H, stride=4), :]
                low, high = mixed(a, b, lane)
                x = starts[c] + e
                s_ref[x, 0:H] = low
                s_ref[x, H:N] = high
                planes.append(low * t_ref[x, 0:H])
                planes.append(high * t_ref[x, H:N])
        buffer[0 : 8 * N] = from_right(jnp.concatenate(planes, axis=0), rz[...])

    def rows(n, buffer):
        for e in range(0, 8, 2):
            x = starts[2 * n + e // 4] + e % 4
            a, b = from_left(ly[...], buffer[e * N : (e + 1) * N], buffer[(e + 1) * N : (e + 2) * N])
            one[pl.ds(x * PITCH, N), :] = a
            one[pl.ds((x + 1) * PITCH, N), :] = b

    pipelined(depth, rows, len(starts) // 2, held)


SHIFTS = ((0, 0), (1, 0), (0, 2), (0, -1), (0, 1), (1, -1), (1, 1), (1, 2))


def chunk_starts():
    tgt = lax.axis_index("tgt")
    z, y, c = tgt // 8, tgt // 2 % 4, tgt % 2
    starts = []
    for dz, dy in SHIFTS:
        for dc in range(2):
            to = ((z + dz) % 2 * 4 + (y + dy + 4) % 4) * 2 + (c + dc) % 2
            starts.append(to * 4)
    return starts


def slab_starts():
    src = lax.axis_index("src")
    x, h = src // 2, src % 2
    starts = []
    for dh in (1, 0):
        for dx in (2, 1, -1, 0):
            starts.append(((x + dx + 4) % 4 * 2 + (h + dh) % 2) * 8)
    return starts


def prepare_kernel(w_ref, raw, *refs):
    tables, (w_out, t_ref, k_ref, *outs), (t_in, sems) = refs[:7], refs[7:17], refs[17:]
    copies = [pltpu.make_async_copy(raw, t_in, sems.at[7])]
    for n, (table, out) in enumerate(zip(tables, outs)):
        copies.append(pltpu.make_async_copy(table, out, sems.at[n]))
    for copy in copies:
        copy.start()
    half = lax.broadcasted_iota(jnp.int32, (8, L), 1) < N
    w_out[...] = jnp.where(half, -w_ref[0], -w_ref[1])
    lane = lane_mask()

    row = lax.broadcasted_iota(jnp.int32, (N, L), 0)
    column = lax.broadcasted_iota(jnp.int32, (N, L), 1) % N
    x = jnp.where(row > H, row - H, row).astype(jnp.float32)
    z = jnp.where(column > H, column - H, column).astype(jnp.float32)
    base = x * x + z * z + 0.25

    def body(y, _):
        k_ref[y] = 16.0 / (base + (y * y).astype(jnp.float32))
        return 0

    lax.fori_loop(0, H + 1, body, 0, unroll=3)
    for copy in copies:
        copy.wait()

    def target(x, _):
        t = t_in[pl.ds(x // 8 * SLAB + x % 8, H, stride=8), :]
        moved = pltpu.roll(t, N, axis=1)
        t_ref[x, 0:H] = jnp.where(lane, t, moved)
        t_ref[x, H:N] = jnp.where(lane, moved, t)
        return 0

    lax.fori_loop(0, N, target, 0, unroll=8)


def late_kernel(*refs):
    chunks, refs = refs[:16], refs[16:]
    w_ref, t_ref, k_ref, ly, lx, ix, iy, rz, qz = refs[:9]
    outs, (s_ref, one, two, *held) = refs[9:17], refs[17:]
    near_transforms(chunks, chunk_starts(), t_ref, s_ref, one, held, ly, rz)

    def planes(n, buffer):
        for e in range(0, BLOCK, 2):
            y = BLOCK * n + e
            a, b = from_left(
                lx[...],
                one[pl.ds(y, N, stride=PITCH), :],
                one[pl.ds(y + 1, N, stride=PITCH), :],
            )
            buffer[e * N : (e + 1) * N] = a * k_ref[y if y <= H else y - H]
            buffer[(e + 1) * N : (e + 2) * N] = b * k_ref[y + 1 if y < H else y + 1 - H]

    def planes_back(n, buffer):
        for e in range(0, BLOCK, 2):
            y = BLOCK * n + e
            a, b = from_left(ix[...], buffer[e * N : (e + 1) * N], buffer[(e + 1) * N : (e + 2) * N])
            two[pl.ds(y * PITCH, N), :] = a
            two[pl.ds((y + 1) * PITCH, N), :] = b

    pipelined(planes, planes_back, N // BLOCK, held)

    lane = lane_mask()
    slabs = slab_starts()
    weight = w_ref[0:1]

    def rows_back(n, buffer):
        for e in range(0, BLOCK, 2):
            x = slabs[(BLOCK * n + e) // 8] + e % 8
            a, b = from_left(
                iy[...], two[pl.ds(x, N, stride=PITCH), :], two[pl.ds(x + 1, N, stride=PITCH), :]
            )
            buffer[e * N : (e + 1) * N] = a
            buffer[(e + 1) * N : (e + 2) * N] = b

    def depth_back(n, buffer):
        field = from_right(buffer[...], qz[...])
        for e in range(BLOCK):
            slab = (BLOCK * n + e) // 8
            v = field[e * N : (e + 1) * N] * s_ref[slabs[slab] + e % 8] * weight
            low, high = v[:H], v[H:]
            kept = jnp.where(lane, low, high)
            other = jnp.where(lane, high, low)
            outs[slab][pl.ds(e % 8, H, stride=8), :] = kept + pltpu.roll(other, N, axis=1)

    pipelined(rows_back, depth_back, N // BLOCK, held)


HELD = [pltpu.VMEM((BLOCK * N, L), jnp.float32)] * 2
SMEM = pl.BlockSpec(memory_space=pltpu.SMEM)
ANY = pl.BlockSpec(memory_space=pltpu.HBM)
VMEM = pl.BlockSpec(memory_space=pltpu.VMEM)


def far_off(value):
    return pltpu.with_memory_space_constraint(value, pltpu.HBM)


def near(value):
    return pltpu.with_memory_space_constraint(value, pltpu.VMEM)


def prepare(w, t, own):
    tables = (
        left_table(BASIS_Y),
        left_table(BASIS),
        left_table(BASIS.T),
        left_table(BASIS_Y.T),
        right_table(BASIS.T),
        right_table(BASIS),
    )
    shapes = [((8, L), jnp.float32), ((N, N, L), jnp.float32), ((H + 1, N, L), jnp.float32)]
    shapes += [((CHUNK, L), jnp.float32)] + [(v.shape, jnp.bfloat16) for v in tables]
    return pl.pallas_call(
        prepare_kernel,
        in_specs=[SMEM] + [ANY] * 8,
        out_specs=[VMEM] * 10,
        out_shape=[pltpu.VMEM(*v) for v in shapes],
        scratch_shapes=[pltpu.VMEM((8 * SLAB, L), jnp.float32), pltpu.SemaphoreType.DMA((8,))],
        compiler_params=pltpu.CompilerParams(vmem_limit_bytes=16 << 20),
        name="prepare",
    )(*[far_off(v) for v in (w, t, own, *map(jnp.asarray, tables))])


def late(chunks, prepared):
    return pl.pallas_call(
        late_kernel,
        in_specs=[VMEM] * 25,
        out_specs=[VMEM] * 8,
        out_shape=[pltpu.VMEM((SLAB, L), jnp.float32)] * 8,
        scratch_shapes=[
            pltpu.VMEM((N, N, L), jnp.float32),
            pltpu.VMEM((N * PITCH, L), jnp.float32),
            pltpu.VMEM((N * PITCH, L), jnp.float32),
            *HELD,
        ],
        compiler_params=pltpu.CompilerParams(vmem_limit_bytes=24 << 20),
        name="late",
    )(*[near(v) for v in chunks], *[near(v) for v in prepared])


def tgt_move(value, dz, dy, dc):
    pairs = []
    for z in range(2):
        for y in range(4):
            for c in range(2):
                to = ((z + dz) % 2 * 4 + (y + dy) % 4) * 2 + (c + dc) % 2
                pairs.append(((z * 4 + y) * 2 + c, to))
    return lax.ppermute(value, "tgt", pairs)


def src_move(value, dx, dh):
    pairs = []
    for x in range(4):
        for h in range(2):
            pairs.append((x * 2 + h, (x + dx) % 4 * 2 + (h + dh) % 2))
    return lax.ppermute(value, "src", pairs)


def on_device(targets, sources, occupations):
    own = sources.reshape(2, 4, H, L).transpose(0, 2, 1, 3).reshape(CHUNK, L)
    t = targets.reshape(8, 8, H, L).transpose(0, 2, 1, 3).reshape(8 * SLAB, L)

    across = tgt_move(own, 1, 0, 0)
    far, up, down = (
        tgt_move(own, 0, d, 0) for d in (2, 1, -1)
    )
    sent = [own, across, far, up, down]
    sent += [tgt_move(across, 0, d, 0) for d in (1, -1)]
    sent += [tgt_move(far, 1, 0, 0)]
    other = [tgt_move(v, 0, 0, 1) for v in sent]
    chunks = [v for both in zip(sent, other) for v in both]
    w, t, k, held, *tables = prepare(occupations, t, own)
    parts = late([held, *chunks[1:]], (w, t, k, *tables))

    far = src_move(parts[0], 0, 1)
    up = src_move(parts[1], 1, 0)
    down = src_move(parts[2], -1, 0)
    near = [src_move(parts[5], 1, 0), src_move(parts[6], -1, 0)]
    near.append(src_move(parts[4] + far, 2, 0))
    crossed = src_move(parts[3] + up + down, 0, 1)
    total = lax.optimization_barrier(sum(near, parts[7])) + crossed
    return total.reshape(H, 8, L).transpose(1, 0, 2).reshape(1, 8, H * L)


def solution(mesh):
    return jax.shard_map(
        on_device,
        mesh=mesh,
        in_specs=(P("tgt", None, None), P("src", "tgt", None), P("src")),
        out_specs=P("tgt", "src", None),
        check_vma=False,
    )
```
